256 devices in a mesh: expert: 32 (over z, x), dp: 8 (over y, core).
Axes of the slice: x: 4, y: 4, z: 8, core: 2. Of those that a mesh axis runs over, the one named last changes fastest.
Arguments:
- tokens: bfloat16 [32768, 1024], P(('expert', 'dp')), may hold values from -6 to 6
- cotangent: bfloat16 [32768, 1024], P(('expert', 'dp')), may hold values from -1.5 to 1.5
- expert_ids: int32 [32768, 8], P(('expert', 'dp')), may hold values from 0 to 63, as said below
- route_gates: float32 [32768, 8], P(('expert', 'dp')), may hold values from 0.1 to 1
- pair_swaps: int32 [16], replicated, may hold values from 0 to 999
- gate_up: bfloat16 [64, 1024, 768], P('expert'), may hold values from -0.1875 to 0.1875
- down: bfloat16 [64, 384, 1024], P('expert'), may hold values from -0.3125 to 0.3125
Outputs:
- mixed: bfloat16 [32768, 1024], P(('expert', 'dp'))
- grad_tokens: bfloat16 [32768, 1024], P(('expert', 'dp'))
- moved_gate_up: bfloat16 [64, 1024, 768], P('expert')
- moved_down: bfloat16 [64, 384, 1024], P('expert')
- grad_gate_up: float32 [64, 1024, 768], P('expert', 'dp')
- grad_down: float32 [64, 384, 1024], P('expert', None, 'dp')
The draws below stay inside these ranges and needn't reach their ends.
Inputs may be any that keep to these rules, and one draw needn't show every extreme that they name: `expert_ids`: each row names 8 different experts. In each aligned block of 128 rows no expert is named more than 32 times, and some experts are named exactly 32 times in every block.
All inputs are finite; a program needn't handle non-finite values.
Results may differ from the reference program's by a relative error of at most 0.0064.
Values may be sent and summed in bfloat16 or wider, within the bound.
No kernel may reach another device: no remote copies, remote signals or barrier semaphores. Data moves between devices by JAX's collectives and lax.ppermute only.
A program may use at most 128 MiB of HBM per device.

```python
import math
import jax
import jax.numpy as jnp
from jax import lax

D = 1024
FF = 384
TOPK = 8
TOK_DEV = 128
EXPERTS = 64
TOKENS = 32768
CAP = 32
PAIRS = 16
N_EXPERT = 32


def route_choice(key):
    base = jax.random.fold_in(key, 11)
    blocks = TOKENS // TOK_DEV
    per_block = TOK_DEV * TOPK
    heavy_count = EXPERTS // 4
    rest_count = EXPERTS - heavy_count
    rest_total = per_block - heavy_count * CAP
    low_load = rest_total // rest_count
    spare = rest_total - low_load * rest_count
    limit = min(low_load, CAP - low_load - 1)
    pair_count = rest_count // 2
    expert_order = jax.random.permutation(jax.random.fold_in(base, 1), EXPERTS)

    def one_block(block_key):
        keys = jax.random.split(block_key, 4)
        shuffled = jax.random.permutation(keys[0], rest_count)
        loads = low_load + (jnp.arange(rest_count) < spare).astype(jnp.int32)
        delta = jax.random.randint(keys[1], (pair_count,), 0, limit + 1)
        loads = loads.at[0:2 * pair_count:2].add(delta).at[1:2 * pair_count:2].add(-delta)
        expert_load = jnp.zeros((EXPERTS,), jnp.int32).at[expert_order[:heavy_count]].set(CAP)
        expert_load = expert_load.at[expert_order[heavy_count:][shuffled]].set(loads)
        ends = jnp.cumsum(expert_load)
        spots = jnp.arange(per_block, dtype=jnp.int32)
        expert_of = jnp.sum((ends[None, :] <= spots[:, None]).astype(jnp.int32), axis=1)
        grid = expert_of.reshape(TOPK, TOK_DEV).T
        turn = jax.random.randint(keys[2], (TOK_DEV, 1), 0, TOPK)
        columns = (jnp.arange(TOPK)[None, :] + turn) % TOPK
        grid = jnp.take_along_axis(grid, columns, axis=1)
        return grid[jax.random.permutation(keys[3], TOK_DEV)]
    chosen = jax.vmap(one_block)(jax.random.split(jax.random.fold_in(base, 2), blocks))
    return chosen.reshape(TOKENS, TOPK).astype(jnp.int32)


def draw_expert_ids(key, part):
    return route_choice(key)


def touch_ends(values, stream_key, smallest, high):
    longest = values.shape.index(max(values.shape))
    spots = []
    for shift in (0, 1):
        where = [jax.random.randint(jax.random.fold_in(stream_key, axis), (), 0, length) for axis, length in enumerate(values.shape)]
        where[longest] = (where[longest] + shift) % values.shape[longest]
        spots.append(tuple(where))
    return values.at[spots[0]].set(smallest).at[spots[1]].set(high)


def shard_levels(rng, shape, cuts, smallest, largest):
    def one(dim, parts):
        steps = jax.random.uniform(jax.random.fold_in(jax.random.fold_in(rng, 6), dim), (parts,), jnp.float32, smallest / len(cuts), largest / len(cuts))
        return jnp.repeat(jnp.exp(steps), shape[dim] // parts).reshape((-1,) + (1,) * (len(shape) - dim - 1))

    level = one(*cuts[0])
    for cut in cuts[1:]:
        level = level * one(*cut)
    return level


def centred(key, dims, spread, most, pieces=(), held_as=jnp.bfloat16):
    factor_of = shard_levels(key, dims, pieces, -0.22, 0.18) if pieces else 1.0
    values = jax.random.normal(key, dims, jnp.float32) * spread * factor_of
    return jnp.minimum(jnp.maximum(values, -most), most).astype(held_as)


def setup_inputs(seed: int = 0) -> dict:
    key_list = jax.random.split(jax.random.key(seed), 8)
    return {
        "tokens": centred(key_list[0], (TOKENS, D), 1.0, 6.0, ((0, 256),)),
        "cotangent": centred(key_list[1], (TOKENS, D), 0.25, 1.5, ((0, 256),)),
        "expert_ids": draw_expert_ids(jax.random.fold_in(key_list[7], 71), 0),
        "route_gates": jnp.clip(jnp.exp(math.log(1.0) - 2.3025851 * jax.random.uniform(key_list[3], (TOKENS, TOPK), jnp.float32) ** shard_levels(key_list[3], (TOKENS, TOPK), ((0, 256),), -0.2, 0.2)), 0.1, 1.0),
        "pair_swaps": touch_ends(jax.random.randint(key_list[4], (PAIRS,), 0, 1000), jax.random.fold_in(key_list[4], 1), 0, 999).astype(jnp.int32),
        "gate_up": centred(key_list[5], (EXPERTS, D, 2 * FF), D ** -0.5, 0.1875, ((0, 32),)),
        "down": centred(key_list[6], (EXPERTS, FF, D), FF ** -0.5, 0.3125, ((0, 32),)),
    }


def gated_parts(gate_part):
    sigmoid_gate = jax.nn.sigmoid(gate_part)
    return gate_part * sigmoid_gate, sigmoid_gate


def reference(tokens, cotangent, expert_ids, route_gates, pair_swaps, gate_up, down):
    blocks = TOKENS // TOK_DEV
    routes_total = TOKENS * TOPK
    per_block = TOK_DEV * TOPK
    block_ids = expert_ids.reshape(blocks, per_block).astype(jnp.int32)
    one_hot = (block_ids[:, :, None] == jnp.arange(EXPERTS, dtype=jnp.int32)[None, None, :]).astype(jnp.int32)
    slot_rank = jnp.sum((jnp.cumsum(one_hot, axis=1) - 1) * one_hot, axis=2).astype(jnp.int32)
    block_of = jnp.arange(blocks, dtype=jnp.int32)[:, None] * jnp.ones((1, per_block), jnp.int32)
    position = ((block_ids * blocks + block_of) * CAP + slot_rank).reshape(-1).astype(jnp.int32)
    route_table = jnp.full((EXPERTS * blocks * CAP,), routes_total, jnp.int32)
    route_table = route_table.at[position].set(jnp.arange(routes_total, dtype=jnp.int32))
    route_table = route_table.reshape(EXPERTS, blocks * CAP)
    token_of = jnp.concatenate([jnp.arange(routes_total, dtype=jnp.int32) // TOPK, jnp.full((1,), TOKENS, jnp.int32)])
    padded_tokens = jnp.concatenate([tokens, jnp.zeros((1, D), tokens.dtype)], axis=0)
    padded_cot = jnp.concatenate([cotangent, jnp.zeros((1, D), cotangent.dtype)], axis=0)
    padded_gates = jnp.concatenate([route_gates.reshape(-1), jnp.zeros((1,), route_gates.dtype)])

    def per_expert(totals, inputs):
        mixed_total, grad_total = totals
        route_index, weight_gu, weight_dn = inputs
        token_index = token_of[route_index]
        rows_in = padded_tokens[token_index]
        activation = jnp.dot(rows_in, weight_gu, preferred_element_type=jnp.float32)
        gate_part = activation[:, :FF]
        up_part = activation[:, FF:]
        silu_gate, sigmoid_gate = gated_parts(gate_part)
        inner = (silu_gate * up_part).astype(jnp.bfloat16)
        expert_out = jnp.dot(inner, weight_dn, preferred_element_type=jnp.float32).astype(jnp.bfloat16)
        gate_values = padded_gates[route_index].astype(jnp.float32)
        mixed_total = mixed_total.at[token_index].add(gate_values[:, None] * expert_out.astype(jnp.float32))
        scaled_cot = (gate_values[:, None] * padded_cot[token_index].astype(jnp.float32)).astype(jnp.bfloat16)
        inner_grad = jnp.dot(scaled_cot, weight_dn.T, preferred_element_type=jnp.float32)
        down_grad = jnp.dot(inner.T, scaled_cot, preferred_element_type=jnp.float32)
        gate_grad = inner_grad * up_part * sigmoid_gate * (1.0 + gate_part * (1.0 - sigmoid_gate))
        act_grad = jnp.concatenate([gate_grad, inner_grad * silu_gate], axis=1).astype(jnp.bfloat16)
        gate_up_grad = jnp.dot(rows_in.T, act_grad, preferred_element_type=jnp.float32)
        route_grad = jnp.dot(act_grad, weight_gu.T, preferred_element_type=jnp.float32).astype(jnp.bfloat16)
        grad_total = grad_total.at[token_index].add(route_grad.astype(jnp.float32))
        return (mixed_total, grad_total), (gate_up_grad, down_grad)

    empty = jnp.zeros((TOKENS + 1, D), jnp.float32)
    totals, expert_grads = lax.scan(per_expert, (empty, empty), (route_table, gate_up, down))
    holders = jnp.arange(N_EXPERT, dtype=jnp.int32)
    pair_flag = pair_swaps[holders % PAIRS] % 2
    source = jnp.where(pair_flag > 0, (holders + PAIRS) % N_EXPERT, holders)
    order = jnp.stack([2 * holders, 2 * source + 1], axis=1).reshape(-1).astype(jnp.int32)
    mixed = totals[0][:TOKENS].astype(jnp.bfloat16)
    grad_tokens = totals[1][:TOKENS].astype(jnp.bfloat16)
    return (mixed, grad_tokens, gate_up[order], down[order], expert_grads[0][order], expert_grads[1][order])
```

```python
import functools

import jax
import jax.numpy as jnp
from jax import lax
from jax.experimental import pallas as pl
from jax.experimental.pallas import tpu as pltpu
from jax.sharding import PartitionSpec as P

BF = jnp.bfloat16
F32 = jnp.float32
ROWS = 128
SLOTS = 32
META = 8
NX = 4
NZ = 8
HELD = 4


def nt(a, b):
    return lax.dot_general(a, b, (((1,), (1,)), ((), ())), preferred_element_type=F32)


def tn(a, b):
    return lax.dot_general(a, b, (((0,), (0,)), ((), ())), preferred_element_type=F32)


def nn(a, b):
    return lax.dot_general(a, b, (((1,), (0,)), ((), ())), preferred_element_type=F32)


def layer_kernel(counts, ids_ref, *refs):
    n_in = len(counts)
    blocks = refs[:n_in]
    gu_ref, dn_ref = refs[n_in : n_in + 2]
    part_ref, rows_ref, scaled_ref, inner_ref, act_ref = refs[n_in + 2 : n_in + 7]
    out_scr, back_scr, back_sel, gate_hi, gate_lo = refs[n_in + 7 :]
    e = pl.program_id(0)
    ff = dn_ref.shape[1]
    where = [(ref, j) for ref, count in zip(blocks, counts) for j in range(count)]

    @pl.when(e == 0)
    def _():
        upper = (
            lax.broadcasted_iota(jnp.int32, (ROWS, ROWS), 0)
            <= lax.broadcasted_iota(jnp.int32, (ROWS, ROWS), 1)
        ).astype(BF)
        slot_no = lax.broadcasted_iota(jnp.int32, (SLOTS, ROWS), 0).astype(F32) + 1.0
        for b, (ref, j) in enumerate(where):
            meta = ref[j, 2 * ROWS : 2 * ROWS + META, 0 : 4 * ROWS].astype(F32)
            named = meta[:, 0:ROWS]
            gates = (
                meta[:, ROWS : 2 * ROWS] + meta[:, 2 * ROWS : 3 * ROWS]
            ) + meta[:, 3 * ROWS : 4 * ROWS]
            hits = []
            weights = []
            for h in range(HELD):
                equal = named == ids_ref[h].astype(F32)
                hits.append(jnp.sum(jnp.where(equal, 1.0, 0.0), axis=0, keepdims=True))
                weights.append(jnp.sum(jnp.where(equal, gates, 0.0), axis=0, keepdims=True))
            hit = jnp.concatenate(hits + hits, axis=0)
            rank = nn(hit.astype(BF), upper)
            picks = []
            scales = []
            for h in range(HELD):
                pick = jnp.where(
                    (rank[h : h + 1, :] == slot_no) & (hits[h] > 0.0), 1.0, 0.0
                )
                picks.append(pick)
                scales.append(pick * weights[h])
            select = jnp.concatenate(picks, axis=0)
            scale = jnp.concatenate(scales, axis=0)
            select_bf = select.astype(BF)
            rows = nn(select_bf, ref[j, 0:ROWS, :]).astype(BF)
            cot = nn(select_bf, ref[j, ROWS : 2 * ROWS, :])
            scaled = (jnp.sum(scale, axis=1, keepdims=True) * cot).astype(BF)
            for h in range(HELD):
                rows_ref[h, b * SLOTS : (b + 1) * SLOTS, :] = rows[h * SLOTS : (h + 1) * SLOTS]
                scaled_ref[h, b * SLOTS : (b + 1) * SLOTS, :] = scaled[h * SLOTS : (h + 1) * SLOTS]
            scale_t = scale.T
            high = scale_t.astype(BF)
            back_sel[b] = select.T.astype(BF)
            gate_hi[b] = high
            gate_lo[b] = (scale_t - high.astype(F32)).astype(BF)

    rows_in = rows_ref[e]
    scaled_cot = scaled_ref[e]
    gu = gu_ref[0]
    dn = dn_ref[0]
    activation = nn(rows_in, gu)
    gate_part = activation[:, :ff]
    up_part = activation[:, ff:]
    sigmoid_gate = jax.nn.sigmoid(gate_part)
    silu_gate = gate_part * sigmoid_gate
    inner = (silu_gate * up_part).astype(BF)
    inner_ref[0] = inner
    expert_out = nn(inner, dn).astype(BF)
    inner_grad = nt(scaled_cot, dn)
    gate_grad = inner_grad * up_part * sigmoid_gate * (1.0 + gate_part * (1.0 - sigmoid_gate))
    act_grad = jnp.concatenate([gate_grad, inner_grad * silu_gate], axis=1).astype(BF)
    act_ref[0] = act_grad
    route_grad = nt(act_grad, gu).astype(BF)
    at = pl.ds(pl.multiple_of(e * SLOTS, SLOTS), SLOTS)
    for b in range(len(where)):
        out_scr[b, at, :] = expert_out[b * SLOTS : (b + 1) * SLOTS]
        back_scr[b, at, :] = route_grad[b * SLOTS : (b + 1) * SLOTS]

    @pl.when(e == HELD - 1)
    def _():
        for b in range(len(where)):
            mixed = nn(gate_hi[b], out_scr[b]) + nn(gate_lo[b], out_scr[b])
            part_ref[b, 0:ROWS, :] = mixed.astype(BF)
            part_ref[b, ROWS : 2 * ROWS, :] = nn(back_sel[b], back_scr[b]).astype(BF)


def layer(ids, blocks, gate_up, down):
    counts = tuple(block.shape[0] for block in blocks)
    n = sum(counts)
    width = blocks[0].shape[2]
    ff = down.shape[1]
    routes = n * SLOTS
    whole = lambda shape: pl.BlockSpec(shape, lambda e, ids: (0,) * len(shape))
    one = lambda shape: pl.BlockSpec((1,) + shape[1:], lambda e, ids: (e, 0, 0))
    outs = [
        (n, 2 * ROWS, width),
        (HELD, routes, width),
        (HELD, routes, width),
        (HELD, routes, ff),
        (HELD, routes, 2 * ff),
    ]
    return pl.pallas_call(
        functools.partial(layer_kernel, counts),
        out_shape=[jax.ShapeDtypeStruct(s, BF) for s in outs],
        grid_spec=pltpu.PrefetchScalarGridSpec(
            num_scalar_prefetch=1,
            grid=(HELD,),
            in_specs=[whole(block.shape) for block in blocks]
            + [one(gate_up.shape), one(down.shape)],
            out_specs=[whole(outs[0]), whole(outs[1]), whole(outs[2]), one(outs[3]), one(outs[4])],
            scratch_shapes=[
                pltpu.VMEM((n, HELD * SLOTS, width), BF),
                pltpu.VMEM((n, HELD * SLOTS, width), BF),
                pltpu.VMEM((n, ROWS, HELD * SLOTS), BF),
                pltpu.VMEM((n, ROWS, HELD * SLOTS), BF),
                pltpu.VMEM((n, ROWS, HELD * SLOTS), BF),
            ],
        ),
        compiler_params=pltpu.CompilerParams(dimension_semantics=("arbitrary",)),
        name="layer",
    )(ids, *blocks, gate_up, down)


def grads_kernel(n, *refs):
    rows = jnp.concatenate([r[0] for r in refs[0:n]], axis=0)
    scaled = jnp.concatenate([r[0] for r in refs[n : 2 * n]], axis=0)
    inner = jnp.concatenate([r[0] for r in refs[2 * n : 3 * n]], axis=0)
    act = jnp.concatenate([r[0] for r in refs[3 * n : 4 * n]], axis=0)
    out = refs[4 * n]
    parts = out.shape[0]
    lanes = out.shape[3]
    tiles = act.shape[1] // lanes
    high = rows.shape[1] // parts
    for d in range(parts):
        grad = tn(rows[:, d * high : (d + 1) * high], act).astype(BF)
        for c in range(tiles):
            out[d, 0, c * high : (c + 1) * high, :] = grad[:, c * lanes : (c + 1) * lanes]
    down = tn(inner, scaled).astype(BF)
    for d in range(parts):
        out[d, 0, tiles * high :, :] = down[:, d * lanes : (d + 1) * lanes]


def grads(saved, parts):
    groups = [[s[k] for s in saved] for k in range(4)]
    width = groups[0][0].shape[2]
    ff = groups[2][0].shape[2]
    one = lambda a: pl.BlockSpec((1,) + a.shape[1:], lambda e: (e, 0, 0))
    lanes = width // parts
    shape = (parts, HELD, lanes * (2 * ff // lanes) + ff, lanes)
    flat = [a for g in groups for a in g]
    return pl.pallas_call(
        functools.partial(grads_kernel, len(saved)),
        out_shape=jax.ShapeDtypeStruct(shape, BF),
        grid=(HELD,),
        in_specs=[one(a) for a in flat],
        out_specs=pl.BlockSpec((parts, 1) + shape[2:], lambda e: (0, e, 0, 0)),
        compiler_params=pltpu.CompilerParams(dimension_semantics=("arbitrary",)),
        name="weight_grads",
    )(*flat)


def move(block, dz, dx):
    route = [
        (z * NX + x, (z + dz) % NZ * NX + (x + dx) % NX) for z in range(NZ) for x in range(NX)
    ]
    return lax.ppermute(block, "expert", route)


def total(*arrays):
    acc = arrays[0].astype(F32)
    for a in arrays[1:]:
        acc = acc + a.astype(F32)
    return acc


def shards(tokens, cotangent, expert_ids, route_gates, pair_swaps, gate_up, down):
    devices = lax.axis_size("expert")
    parts = lax.axis_size("dp")
    half_axis = devices // 2
    me = lax.axis_index("expert")
    mine = lax.axis_index("dp")
    width = tokens.shape[1]
    ff = down.shape[1]
    lanes = width // parts
    tiles = 2 * ff // lanes
    swapped = (
        jnp.sum(jnp.where(jnp.arange(half_axis) == me % half_axis, pair_swaps % 2, 0)) > 0
    )

    my_rows = lax.dynamic_slice_in_dim(gate_up, mine * lanes, lanes, axis=1)
    my_cols = lax.dynamic_slice_in_dim(down, mine * lanes, lanes, axis=2)
    share = jnp.concatenate(
        [my_rows[:, :, c * lanes : (c + 1) * lanes] for c in range(tiles)] + [my_cols], axis=1
    )
    theirs = lax.all_gather(move(share, NZ // 2, 0), "dp", axis=0, tiled=False)
    partner_gu = (
        theirs[:, :, : tiles * lanes, :]
        .reshape(parts, 2, tiles, lanes, lanes)
        .transpose(1, 0, 3, 2, 4)
        .reshape(gate_up.shape)
    )
    partner_dn = theirs[:, :, tiles * lanes :, :].transpose(1, 2, 0, 3).reshape(down.shape)
    moved_gate_up = jnp.stack([gate_up[0], jnp.where(swapped, partner_gu[1], gate_up[1])])
    moved_down = jnp.stack([down[0], jnp.where(swapped, partner_dn[1], down[1])])
    held_gu = jnp.concatenate([gate_up, partner_gu], axis=0)
    held_dn = jnp.concatenate([down, partner_dn], axis=0)
    partner = (me + half_axis) % devices
    ids = jnp.stack([2 * me, 2 * me + 1, 2 * partner, 2 * partner + 1]).astype(jnp.int32)

    high = lax.reduce_precision(route_gates, 8, 7)
    rest = route_gates - high
    middle = lax.reduce_precision(rest, 8, 7)
    low = rest - middle
    meta = jnp.concatenate([expert_ids.astype(F32).T, high.T, middle.T, low.T], axis=1)
    meta = jnp.pad(meta.astype(BF), ((0, 0), (0, width - meta.shape[1])))
    block = jnp.concatenate([tokens, cotangent, meta], axis=0)

    near = jnp.stack([block, move(block, 0, 1), move(block, 0, -1), move(block, 0, 2)])
    above = move(near, 1, 0)
    below = move(near, -1, 0)
    far_above = move(above[:2], 1, 0)
    far_below = move(below[2:], -1, 0)

    near_part, *near_saved = layer(ids, [near], held_gu, held_dn)
    next_part, *next_saved = layer(ids, [above, below], held_gu, held_dn)
    far_part, *far_saved = layer(ids, [far_above, far_below], held_gu, held_dn)

    back_above = move(far_part[:2], -1, 0)
    back_below = move(far_part[2:], 1, 0)
    send_above = jnp.concatenate([total(next_part[0:2], back_above).astype(BF), next_part[2:4]])
    send_below = jnp.concatenate([next_part[4:6], total(next_part[6:8], back_below).astype(BF)])
    sums = total(near_part, move(send_above, -1, 0), move(send_below, 1, 0)).astype(BF)
    result = total(
        sums[0], move(sums[1], 0, -1), move(sums[2], 0, 1), move(sums[3], 0, 2)
    ).astype(BF)
    mixed = result[:ROWS]
    grad_tokens = result[ROWS:]

    weight_grads = grads([near_saved, next_saved, far_saved], parts)
    mine_of = lax.psum_scatter(weight_grads, "dp", scatter_dimension=0, tiled=False)
    give = jnp.stack([mine_of[2], jnp.where(swapped, mine_of[1], mine_of[3])])
    keep = jnp.stack([mine_of[0], jnp.where(swapped, mine_of[3], mine_of[1])])
    summed = total(keep, move(give, NZ // 2, 0))
    grad_gate_up = (
        summed[:, : tiles * lanes, :]
        .reshape(2, tiles, lanes, lanes)
        .transpose(0, 2, 1, 3)
        .reshape(2, lanes, 2 * ff)
    )
    grad_down = summed[:, tiles * lanes :, :]
    return (mixed, grad_tokens, moved_gate_up, moved_down, grad_gate_up, grad_down)


def solution(mesh):
    in_specs = (
        P(("expert", "dp"), None),
        P(("expert", "dp"), None),
        P(("expert", "dp"), None),
        P(("expert", "dp"), None),
        P(),
        P("expert", None, None),
        P("expert", None, None),
    )
    out_specs = (
        P(("expert", "dp"), None),
        P(("expert", "dp"), None),
        P("expert", None, None),
        P("expert", None, None),
        P("expert", "dp", None),
        P("expert", None, "dp"),
    )
    return jax.shard_map(shards, mesh=mesh, in_specs=in_specs, out_specs=out_specs, check_vma=False)
```

```python
import functools

import jax
import jax.numpy as jnp
from jax import lax
from jax.experimental import pallas as pl
from jax.experimental.pallas import tpu as pltpu
from jax.sharding import PartitionSpec as P


BF = jnp.bfloat16
F32 = jnp.float32
ROWS = 128
SLOTS = 32
META = 8
NX = 4
NZ = 8
PAIR = 2


def nt(a, b):
    return lax.dot_general(a, b, (((1,), (1,)), ((), ())), preferred_element_type=F32)


def tn(a, b):
    return lax.dot_general(a, b, (((0,), (0,)), ((), ())), preferred_element_type=F32)


def nn(a, b):
    return lax.dot_general(a, b, (((1,), (0,)), ((), ())), preferred_element_type=F32)


NEAR, SIDE, FAR = 4, 4, 2
BLOCKS = NEAR + 2 * SIDE + 2 * FAR


def constants():
    upper = lax.broadcasted_iota(jnp.int32, (ROWS, ROWS), 0) <= lax.broadcasted_iota(
        jnp.int32, (ROWS, ROWS), 1
    )
    slot_no = lax.broadcasted_iota(jnp.int32, (SLOTS, ROWS), 0).astype(F32) + 1.0
    return upper.astype(BF), slot_no


def picks_of(meta, ids_ref, experts, upper, slot_no):
    meta = meta.astype(F32)
    named = meta[:, 0:ROWS]
    gates = (meta[:, ROWS : 2 * ROWS] + meta[:, 2 * ROWS : 3 * ROWS]) + meta[:, 3 * ROWS :]
    hits = []
    weights = []
    for h in experts:
        equal = named == ids_ref[h].astype(F32)
        hits.append(jnp.sum(jnp.where(equal, 1.0, 0.0), axis=0, keepdims=True))
        weights.append(jnp.sum(jnp.where(equal, gates, 0.0), axis=0, keepdims=True))
    rank = nn(jnp.concatenate(hits * (8 // len(hits)), axis=0).astype(BF), upper)
    picks = [
        jnp.where((rank[h : h + 1, :] == slot_no) & (hit > 0.0), 1.0, 0.0)
        for h, hit in enumerate(hits)
    ]
    scales = [pick * weight for pick, weight in zip(picks, weights)]
    return jnp.concatenate(picks, axis=0), jnp.concatenate(scales, axis=0)


def experts_of(rows_in, scaled_cot, gu, dn):
    ff = dn.shape[0]
    activation = nn(rows_in, gu)
    inner_grad = nt(scaled_cot, dn)
    gate_part = activation[:, :ff]
    up_part = activation[:, ff:]
    sigmoid_gate = jax.nn.sigmoid(gate_part)
    silu_gate = gate_part * sigmoid_gate
    inner = (silu_gate * up_part).astype(BF)
    expert_out = nn(inner, dn).astype(BF)
    gate_grad = inner_grad * up_part * sigmoid_gate * (1.0 + gate_part * (1.0 - sigmoid_gate))
    act_grad = jnp.concatenate([gate_grad, inner_grad * silu_gate], axis=1).astype(BF)
    route_grad = nt(act_grad, gu).astype(BF)
    return inner, expert_out, act_grad, route_grad


def first_kernel(counts, cot_at, n_cots, ids_ref, *refs):
    token_refs = refs[: len(counts)]
    cots = refs[len(counts) : len(counts) + n_cots]
    refs = refs[len(counts) + n_cots :]
    gu_ref, dn_ref, out_ref, back_ref, rows_ref, scaled_ref = refs[:6]
    sel_ref, high_ref, low_ref, inner_ref, act_ref = refs[6:]
    e = pl.program_id(0)
    tokens_at = [(ref, j) for ref, count in zip(token_refs, counts) for j in range(count)]

    @pl.when(e == 0)
    def _():
        upper, slot_no = constants()
        for b, (ref, j) in enumerate(tokens_at):
            meta = ref[j, ROWS : ROWS + META, 0 : 4 * ROWS]
            select, scale = picks_of(meta, ids_ref, range(2 * PAIR), upper, slot_no)
            select_bf = select.astype(BF)
            k, i = cot_at[b]
            cot_rows = cots[k][...] if i is None else cots[k][i]
            rows = nn(select_bf, ref[j, 0:ROWS, :]).astype(BF)
            cot = nn(select_bf, cot_rows)
            scaled = (jnp.sum(scale, axis=1, keepdims=True) * cot).astype(BF)
            for h in range(2 * PAIR):
                rows_ref[h, b * SLOTS : (b + 1) * SLOTS, :] = rows[h * SLOTS : (h + 1) * SLOTS]
                scaled_ref[h, b * SLOTS : (b + 1) * SLOTS, :] = scaled[h * SLOTS : (h + 1) * SLOTS]
            scale_t = scale.T
            high = scale_t.astype(BF)
            sel_ref[b] = select.T.astype(BF)
            high_ref[b] = high
            low_ref[b] = (scale_t - high.astype(F32)).astype(BF)

    inner, expert_out, act_grad, route_grad = experts_of(
        rows_ref[e], scaled_ref[e], gu_ref[0], dn_ref[0]
    )
    inner_ref[0] = inner
    act_ref[0] = act_grad
    for b in range(len(tokens_at)):
        out_ref[b] = expert_out[b * SLOTS : (b + 1) * SLOTS]
        back_ref[b] = route_grad[b * SLOTS : (b + 1) * SLOTS]


def one_at(a, shift=0):
    return pl.BlockSpec((1,) + a.shape[1:], lambda e, *_: (e + shift, 0, 0))


def struct(*shape):
    return jax.ShapeDtypeStruct(shape, BF)


def first_layer(ids, tokens, cots, cot_at, gate_up, down):
    width = tokens[0].shape[2]
    ff = down.shape[1]
    counts = tuple(a.shape[0] for a in tokens)
    n = sum(counts)
    routes = n * SLOTS
    whole = lambda a: pl.BlockSpec(
        a.shape, lambda e, ids: (0,) * len(a.shape), pipeline_mode=pl.Buffered(1)
    )
    kept = lambda a: pl.BlockSpec(a.shape, lambda e, ids: (0,) * len(a.shape))
    slots = pl.BlockSpec((n, SLOTS, width), lambda e, ids: (0, e, 0))
    by_slot = struct(n, PAIR * SLOTS, width)
    by_expert = struct(2 * PAIR, routes, width)
    turned = struct(n, ROWS, 2 * PAIR * SLOTS)
    inner = struct(PAIR, routes, ff)
    act = struct(PAIR, routes, 2 * ff)
    return pl.pallas_call(
        functools.partial(first_kernel, counts, cot_at, len(cots)),
        out_shape=[by_slot, by_slot, by_expert, by_expert, turned, turned, turned, inner, act],
        grid_spec=pltpu.PrefetchScalarGridSpec(
            num_scalar_prefetch=1,
            grid=(PAIR,),
            in_specs=[whole(a) for a in (*tokens, *cots)] + [one_at(gate_up), one_at(down)],
            out_specs=[slots, slots, kept(by_expert), kept(by_expert)]
            + [kept(turned)] * 3
            + [one_at(inner), one_at(act)],
        ),
        compiler_params=pltpu.CompilerParams(dimension_semantics=("arbitrary",)),
        name="first_layer",
    )(ids, *tokens, *cots, gate_up, down)


def last_kernel(n, *refs):
    rows = jnp.concatenate([ref[0] for ref in refs[:n]], axis=0)
    scaled = jnp.concatenate([ref[0] for ref in refs[n : 2 * n]], axis=0)
    gu_ref, dn_ref, out_ref, back_ref, inner_ref, act_ref = refs[2 * n :]
    inner, expert_out, act_grad, route_grad = experts_of(rows, scaled, gu_ref[0], dn_ref[0])
    inner_ref[0] = inner
    act_ref[0] = act_grad
    for b in range(BLOCKS):
        out_ref[b] = expert_out[b * SLOTS : (b + 1) * SLOTS]
        back_ref[b] = route_grad[b * SLOTS : (b + 1) * SLOTS]


def last_layer(rows, scaled, gate_up, down):
    width = gate_up.shape[1]
    ff = down.shape[1]
    routes = BLOCKS * SLOTS
    slots = pl.BlockSpec((BLOCKS, SLOTS, width), lambda e: (0, e, 0))
    by_slot = struct(BLOCKS, PAIR * SLOTS, width)
    inner = struct(PAIR, routes, ff)
    act = struct(PAIR, routes, 2 * ff)
    return pl.pallas_call(
        functools.partial(last_kernel, len(rows)),
        out_shape=[by_slot, by_slot, inner, act],
        grid=(PAIR,),
        in_specs=[one_at(a, PAIR) for a in (*rows, *scaled)] + [one_at(gate_up), one_at(down)],
        out_specs=[slots, slots, one_at(inner), one_at(act)],
        compiler_params=pltpu.CompilerParams(dimension_semantics=("arbitrary",)),
        name="last_layer",
    )(*rows, *scaled, gate_up, down)


MIXED = (("near", 4), ("above_far", 2), ("above", 2), ("below", 2), ("below_far", 2), ("far", 2), ("far", 2))


def combine_kernel(*refs):
    main, rest, partner = refs[:5], refs[5:10], refs[10:12]
    mixed_refs = refs[12 : 12 + len(MIXED)]
    grad_refs = refs[12 + len(MIXED) :]
    mixed_at = [(ref, j) for ref, (_, count) in zip(mixed_refs, MIXED) for j in range(count)]
    for group in range(4):

        @pl.when(pl.program_id(0) == group)
        def _():
            outs, backs, sels, highs, lows = main if group < 3 else rest
            for j in range(4):
                out = jnp.concatenate([outs[j], partner[0][j]], axis=0)
                back = jnp.concatenate([backs[j], partner[1][j]], axis=0)
                ref, i = mixed_at[4 * group + j]
                ref[i] = (nn(highs[j], out) + nn(lows[j], out)).astype(BF)
                grad_refs[NX * (0, 1, 1, 2)[group] + j][0] = nn(sels[j], back).astype(BF)


def combine(main, rest, partner):
    width = partner[0].shape[2]
    some = lambda a: pl.BlockSpec((4,) + a.shape[1:], lambda g: (jnp.minimum(g, 2), 0, 0))
    once = lambda a: pl.BlockSpec(a.shape, lambda g: (0, 0, 0))
    each = lambda a: pl.BlockSpec((4,) + a.shape[1:], lambda g: (g, 0, 0))
    shapes = [struct(count, ROWS, width) for _, count in MIXED]
    grads_of = [struct(1, ROWS, width), struct(2, ROWS, width), struct(1, ROWS, width)]
    return pl.pallas_call(
        combine_kernel,
        out_shape=shapes + [a for a in grads_of for _ in range(NX)],
        grid=(4,),
        in_specs=[some(a) for a in main] + [once(a) for a in rest] + [each(a) for a in partner],
        out_specs=[once(a) for a in shapes]
        + [once(grads_of[0])] * NX
        + [pl.BlockSpec((1, ROWS, width), lambda g: (jnp.clip(g - 1, 0, 1), 0, 0))] * NX
        + [once(grads_of[2])] * NX,
        compiler_params=pltpu.CompilerParams(dimension_semantics=("arbitrary",)),
        name="combine",
    )(*main, *rest, *partner)


def grads_kernel(counts, *refs):
    groups = []
    for count in counts:
        groups.append(jnp.concatenate([ref[0] for ref in refs[:count]], axis=0))
        refs = refs[count:]
    rows, scaled, inner, act = groups
    out = refs[-1]
    parts = out.shape[0]
    lanes = out.shape[3]
    tiles = act.shape[1] // lanes
    high = rows.shape[1] // parts
    for d in range(0, parts, 2):
        grad = tn(rows[:, d * high : (d + 2) * high], act).astype(BF)
        for p in range(2):
            for c in range(tiles):
                out[d + p, 0, c * high : (c + 1) * high, :] = grad[
                    p * high : (p + 1) * high, c * lanes : (c + 1) * lanes
                ]
    down = tn(inner, scaled).astype(BF)
    for d in range(parts):
        out[d, 0, tiles * high :, :] = down[:, d * lanes : (d + 1) * lanes]


def grads(rows, scaled, inner, act, parts, first, into=None):
    width = rows[0].shape[2]
    ff = inner[0].shape[2]
    lanes = width // parts
    shape = (parts, 2 * PAIR, lanes * (2 * ff // lanes) + ff, lanes)
    more = [] if into is None else [into]
    operands = [*rows, *scaled, *inner, *act]
    return pl.pallas_call(
        functools.partial(grads_kernel, (len(rows), len(scaled), len(inner), len(act))),
        out_shape=struct(*shape),
        grid=(PAIR,),
        in_specs=[one_at(a, first) for a in (*rows, *scaled)]
        + [one_at(a) for a in (*inner, *act)]
        + [pl.BlockSpec(memory_space=pl.ANY)] * len(more),
        out_specs=pl.BlockSpec((parts, 1) + shape[2:], lambda e: (0, e + first, 0, 0)),
        input_output_aliases={len(operands): 0} if more else {},
        compiler_params=pltpu.CompilerParams(dimension_semantics=("arbitrary",)),
        name="weight_grads",
    )(*operands, *more)


def share_kernel(part_ref, gu_ref, dn_ref, out_ref):
    lanes = out_ref.shape[2]
    tiles = gu_ref.shape[2] // lanes
    high = gu_ref.shape[1]
    for c in range(tiles):
        out_ref[0, c * high : (c + 1) * high, :] = gu_ref[0, :, c * lanes : (c + 1) * lanes]
    out_ref[0, tiles * high :, :] = dn_ref[0]


def share_of(part, gate_up, down, parts):
    lanes = down.shape[2] // parts
    high = gate_up.shape[1] // parts
    rows = high * (gate_up.shape[2] // lanes) + down.shape[1]
    return pl.pallas_call(
        share_kernel,
        out_shape=jax.ShapeDtypeStruct((PAIR, rows, lanes), BF),
        grid_spec=pltpu.PrefetchScalarGridSpec(
            num_scalar_prefetch=1,
            grid=(PAIR,),
            in_specs=[
                pl.BlockSpec((1, high, gate_up.shape[2]), lambda e, part: (e, part[0], 0)),
                pl.BlockSpec((1, down.shape[1], lanes), lambda e, part: (e, 0, part[0])),
            ],
            out_specs=pl.BlockSpec((1, rows, lanes), lambda e, part: (e, 0, 0)),
        ),
        name="share",
    )(part, gate_up, down)


def whole_kernel(in_ref, gu_ref, dn_ref):
    parts = in_ref.shape[0]
    lanes = in_ref.shape[3]
    tiles = gu_ref.shape[2] // lanes
    high = gu_ref.shape[1] // parts
    for d in range(parts):
        for c in range(tiles):
            gu_ref[0, d * high : (d + 1) * high, c * lanes : (c + 1) * lanes] = in_ref[
                d, 0, c * high : (c + 1) * high, :
            ]
        dn_ref[0, :, d * lanes : (d + 1) * lanes] = in_ref[d, 0, tiles * high :, :]


def whole_of(pieces, gate_up, down):
    parts, _, rows, lanes = pieces.shape
    one = lambda shape: pl.BlockSpec((1,) + shape[1:], lambda e: (e, 0, 0))
    return pl.pallas_call(
        whole_kernel,
        out_shape=[jax.ShapeDtypeStruct(a.shape, BF) for a in (gate_up, down)],
        grid=(PAIR,),
        in_specs=[pl.BlockSpec((parts, 1, rows, lanes), lambda e: (0, e, 0, 0))],
        out_specs=[one(gate_up.shape), one(down.shape)],
        name="whole",
    )(pieces)


def finish_kernel(flag_ref, mine_ref, got_ref, gu_ref, dn_ref):
    lanes = gu_ref.shape[1]
    tiles = gu_ref.shape[2] // lanes
    for s in range(PAIR):
        if s == 0:
            keep = mine_ref[0].astype(F32)
        else:
            swapped = flag_ref[0] > 0
            keep = jnp.where(swapped, mine_ref[PAIR + 1].astype(F32), mine_ref[1].astype(F32))
        grad = keep + got_ref[s].astype(F32)
        for c in range(tiles):
            gu_ref[s, :, c * lanes : (c + 1) * lanes] = grad[c * lanes : (c + 1) * lanes, :]
        dn_ref[s] = grad[tiles * lanes :, :]


def finish(flag, mine_of, got, ff):
    lanes = got.shape[2]
    return pl.pallas_call(
        finish_kernel,
        out_shape=[
            jax.ShapeDtypeStruct((PAIR, lanes, 2 * ff), F32),
            jax.ShapeDtypeStruct((PAIR, ff, lanes), F32),
        ],
        in_specs=[
            pl.BlockSpec(memory_space=pltpu.SMEM),
            pl.BlockSpec(memory_space=pltpu.VMEM),
            pl.BlockSpec(memory_space=pltpu.VMEM),
        ],
        out_specs=[pl.BlockSpec(memory_space=pltpu.VMEM)] * 2,
        name="finish",
    )(flag, mine_of, got)


AROUND = (1, -1, 2)


def move(block, dz, dx):
    route = [
        (z * NX + x, (z + dz) % NZ * NX + (x + dx) % NX) for z in range(NZ) for x in range(NX)
    ]
    return lax.ppermute(block, "expert", route)


def total(*arrays):
    acc = arrays[0].astype(F32)
    for a in arrays[1:]:
        acc = acc + a.astype(F32)
    return acc


def step(tokens, cotangent, expert_ids, route_gates, pair_swaps, gate_up, down):
    devices = lax.axis_size("expert")
    parts = lax.axis_size("dp")
    half_axis = devices // 2
    me = lax.axis_index("expert")
    width = tokens.shape[1]
    ff = down.shape[1]
    swapped = (
        jnp.sum(jnp.where(jnp.arange(half_axis) == me % half_axis, pair_swaps % 2, 0)) > 0
    )
    flag = swapped.astype(jnp.int32).reshape(1)
    partner = (me + half_axis) % devices
    ids = jnp.stack([2 * me, 2 * me + 1, 2 * partner, 2 * partner + 1]).astype(jnp.int32)

    cot_up = move(cotangent, 1, 0)
    cot_down = move(cotangent, -1, 0)
    cot_near = [move(cotangent, 0, dx) for dx in AROUND]

    part = lax.axis_index("dp").astype(jnp.int32).reshape(1)
    share = move(share_of(part, gate_up, down, parts), NZ // 2, 0)
    pieces = lax.all_gather(share, "dp", axis=0, tiled=False)

    high = lax.reduce_precision(route_gates, 8, 7)
    rest = route_gates - high
    middle = lax.reduce_precision(rest, 8, 7)
    low = rest - middle
    meta = jnp.concatenate([expert_ids.astype(F32).T, high.T, middle.T, low.T], axis=1)
    meta = jnp.pad(meta.astype(BF), ((0, 0), (0, width - meta.shape[1])))
    block = jnp.concatenate([tokens, meta], axis=0)
    near = jnp.stack([block] + [move(block, 0, dx) for dx in AROUND])
    above = move(near, 1, 0)
    below = move(near, -1, 0)
    far_above = move(above[:FAR], 1, 0)
    far_below = move(below[FAR:], -1, 0)

    cot_far_up = move(cot_up, 1, 0)
    cot_far_down = move(cot_down, -1, 0)
    to_right = jnp.stack([cot_up, cot_down, cot_far_up])
    to_left = jnp.stack([cot_up, cot_down, cot_far_down])
    cot_side = [move(to_right, 0, 1), move(to_left, 0, -1), move(to_left, 0, 2)]
    cots = [cotangent, cot_up, cot_down, cot_far_up, *cot_near, *cot_side]
    cot_at = (
        [(0, None), (4, None), (5, None), (6, None)]
        + [(1, None), (7, 0), (8, 0), (9, 0)]
        + [(2, None), (7, 1), (8, 1), (9, 1)]
    )
    far_cots = [cot_far_up, *cot_side]
    far_at = [(0, None), (1, 2), (2, 2), (3, 2)]

    out1, back1, rows1, scaled1, sel1, high1, low1, inner1, act1 = first_layer(
        ids, [near, above, below], cots, cot_at, gate_up, down
    )
    out2, back2, rows2, scaled2, sel2, high2, low2, inner2, act2 = first_layer(
        ids, [far_above, far_below], far_cots, far_at, gate_up, down
    )
    rows, scaled = (rows1, rows2), (scaled1, scaled2)
    weight_grads = grads(rows, scaled, (inner1, inner2), (act1, act2), parts, 0)
    partner_gu, partner_dn = whole_of(pieces, gate_up, down)
    out3, back3, inner3, act3 = last_layer(rows, scaled, partner_gu, partner_dn)
    weight_grads = grads(rows, scaled, (inner3,), (act3,), parts, PAIR, weight_grads)
    mine_of = lax.psum_scatter(weight_grads, "dp", scatter_dimension=0, tiled=False)
    results = combine(
        (out1, back1, sel1, high1, low1), (out2, back2, sel2, high2, low2), (out3, back3)
    )
    near_grads, side_grads, far_grads = (
        results[k : k + NX] for k in range(len(MIXED), len(MIXED) + 3 * NX, NX)
    )

    home = ((1, -1), (2, 1), (3, 2))
    near_back, side_back, far_back = (
        [move(part[k], 0, dx) for k, dx in home]
        for part in (near_grads, side_grads, far_grads)
    )
    near_mix, up_late, up_now, down_now, down_late, far_up, far_down = results[: len(MIXED)]
    back_up = move(far_up, -1, 0)
    back_down = move(far_down, 1, 0)
    up_now = move(up_now, -1, 0)
    down_now = move(down_now, 1, 0)
    up_late = move(total(up_late, back_up).astype(BF), -1, 0)
    down_late = move(total(down_late, back_down).astype(BF), 1, 0)
    low = total(near_mix[:FAR], up_late, down_now)
    top = total(near_mix[FAR:], up_now, down_late)
    mixed = (
        low[0]
        + move(low[1].astype(BF), 0, -1).astype(F32)
        + move(top[0].astype(BF), 0, 1).astype(F32)
        + move(top[1].astype(BF), 0, 2).astype(F32)
    ).astype(BF)

    grad_far_up = move(total(far_grads[0][0], far_back[0][0]).astype(BF), -1, 0)
    grad_far_down = move(total(far_back[1][0], far_back[2][0]).astype(BF), 1, 0)
    sides = [side_grads[0], *side_back]
    grad_up = total(*[a[0] for a in sides], grad_far_up).astype(BF)
    grad_down_z = total(*[a[1] for a in sides], grad_far_down).astype(BF)
    grad_tokens = total(
        near_grads[0][0], *[a[0] for a in near_back], move(grad_up, -1, 0), move(grad_down_z, 1, 0)
    ).astype(BF)

    moved_gate_up = jnp.stack([gate_up[0], jnp.where(swapped, partner_gu[1], gate_up[1])])
    moved_down = jnp.stack([down[0], jnp.where(swapped, partner_dn[1], down[1])])

    give = jnp.stack([mine_of[PAIR], jnp.where(swapped, mine_of[1], mine_of[PAIR + 1])])
    got = move(give, NZ // 2, 0)
    grad_gate_up, grad_down = finish(flag, mine_of, got, ff)
    return (mixed, grad_tokens, moved_gate_up, moved_down, grad_gate_up, grad_down)


def solution(mesh):
    in_specs = (
        P(("expert", "dp"), None),
        P(("expert", "dp"), None),
        P(("expert", "dp"), None),
        P(("expert", "dp"), None),
        P(),
        P("expert", None, None),
        P("expert", None, None),
    )
    out_specs = (
        P(("expert", "dp"), None),
        P(("expert", "dp"), None),
        P("expert", None, None),
        P("expert", None, None),
        P("expert", "dp", None),
        P("expert", None, "dp"),
    )
    return jax.shard_map(step, mesh=mesh, in_specs=in_specs, out_specs=out_specs, check_vma=False)
```

```python
import functools

import jax
import jax.numpy as jnp
from jax import lax
from jax.experimental import pallas as pl
from jax.experimental.pallas import tpu as pltpu
from jax.sharding import PartitionSpec as P


BF = jnp.bfloat16
F32 = jnp.float32
ROWS = 128
SLOTS = 32
META = 8
NX = 4
NZ = 8
PAIR = 2


def nt(a, b):
    return lax.dot_general(a, b, (((1,), (1,)), ((), ())), preferred_element_type=F32)


def tn(a, b):
    return lax.dot_general(a, b, (((0,), (0,)), ((), ())), preferred_element_type=F32)


def nn(a, b):
    return lax.dot_general(a, b, (((1,), (0,)), ((), ())), preferred_element_type=F32)


NEAR, SIDE, FAR = 4, 4, 2
BLOCKS = NEAR + 2 * SIDE + 2 * FAR


def constants():
    upper = lax.broadcasted_iota(jnp.int32, (ROWS, ROWS), 0) <= lax.broadcasted_iota(
        jnp.int32, (ROWS, ROWS), 1
    )
    slot_no = lax.broadcasted_iota(jnp.int32, (SLOTS, ROWS), 0).astype(F32) + 1.0
    return upper.astype(BF), slot_no


def picks_of(meta, ids_ref, experts, upper, slot_no):
    meta = meta.astype(F32)
    named = meta[:, 0:ROWS]
    gates = (meta[:, ROWS : 2 * ROWS] + meta[:, 2 * ROWS : 3 * ROWS]) + meta[:, 3 * ROWS :]
    hits = []
    weights = []
    for h in experts:
        equal = named == ids_ref[h].astype(F32)
        hits.append(jnp.sum(jnp.where(equal, 1.0, 0.0), axis=0, keepdims=True))
        weights.append(jnp.sum(jnp.where(equal, gates, 0.0), axis=0, keepdims=True))
    rank = nn(jnp.concatenate(hits * (8 // len(hits)), axis=0).astype(BF), upper)
    picks = [
        jnp.where((rank[h : h + 1, :] == slot_no) & (hit > 0.0), 1.0, 0.0)
        for h, hit in enumerate(hits)
    ]
    scales = [pick * weight for pick, weight in zip(picks, weights)]
    return jnp.concatenate(picks, axis=0), jnp.concatenate(scales, axis=0)


def experts_of(rows_in, scaled_cot, gu, dn):
    ff = dn.shape[0]
    activation = nn(rows_in, gu)
    inner_grad = nt(scaled_cot, dn)
    gate_part = activation[:, :ff]
    up_part = activation[:, ff:]
    sigmoid_gate = jax.nn.sigmoid(gate_part)
    silu_gate = gate_part * sigmoid_gate
    inner = (silu_gate * up_part).astype(BF)
    expert_out = nn(inner, dn).astype(BF)
    gate_grad = inner_grad * up_part * sigmoid_gate * (1.0 + gate_part * (1.0 - sigmoid_gate))
    act_grad = jnp.concatenate([gate_grad, inner_grad * silu_gate], axis=1).astype(BF)
    route_grad = nt(act_grad, gu).astype(BF)
    return inner, expert_out, act_grad, route_grad


def first_kernel(counts, cot_at, n_cots, ids_ref, *refs):
    token_refs = refs[: len(counts)]
    cots = refs[len(counts) : len(counts) + n_cots]
    refs = refs[len(counts) + n_cots :]
    gu_ref, dn_ref, out_ref, back_ref, rows_ref, scaled_ref = refs[:6]
    sel_ref, high_ref, low_ref, inner_ref, act_ref = refs[6:]
    e = pl.program_id(0)
    tokens_at = [(ref, j) for ref, count in zip(token_refs, counts) for j in range(count)]

    @pl.when(e == 0)
    def _():
        upper, slot_no = constants()
        for b, (ref, j) in enumerate(tokens_at):
            meta = ref[j, ROWS : ROWS + META, 0 : 4 * ROWS]
            select, scale = picks_of(meta, ids_ref, range(2 * PAIR), upper, slot_no)
            select_bf = select.astype(BF)
            k, i = cot_at[b]
            cot_rows = cots[k][...] if i is None else cots[k][i]
            rows = nn(select_bf, ref[j, 0:ROWS, :]).astype(BF)
            cot = nn(select_bf, cot_rows)
            scaled = (jnp.sum(scale, axis=1, keepdims=True) * cot).astype(BF)
            for h in range(2 * PAIR):
                rows_ref[h, b * SLOTS : (b + 1) * SLOTS, :] = rows[h * SLOTS : (h + 1) * SLOTS]
                scaled_ref[h, b * SLOTS : (b + 1) * SLOTS, :] = scaled[h * SLOTS : (h + 1) * SLOTS]
            scale_t = scale.T
            high = scale_t.astype(BF)
            sel_ref[b] = select.T.astype(BF)
            high_ref[b] = high
            low_ref[b] = (scale_t - high.astype(F32)).astype(BF)

    inner, expert_out, act_grad, route_grad = experts_of(
        rows_ref[e], scaled_ref[e], gu_ref[0], dn_ref[0]
    )
    inner_ref[0] = inner
    act_ref[0] = act_grad
    for b in range(len(tokens_at)):
        out_ref[b] = expert_out[b * SLOTS : (b + 1) * SLOTS]
        back_ref[b] = route_grad[b * SLOTS : (b + 1) * SLOTS]


def one_at(a, shift=0):
    return pl.BlockSpec((1,) + a.shape[1:], lambda e, *_: (e + shift, 0, 0))


def struct(*shape):
    return jax.ShapeDtypeStruct(shape, BF)


def first_layer(ids, tokens, cots, cot_at, gate_up, down):
    width = tokens[0].shape[2]
    ff = down.shape[1]
    counts = tuple(a.shape[0] for a in tokens)
    n = sum(counts)
    routes = n * SLOTS
    whole = lambda a: pl.BlockSpec(
        a.shape, lambda e, ids: (0,) * len(a.shape), pipeline_mode=pl.Buffered(1)
    )
    kept = lambda a: pl.BlockSpec(a.shape, lambda e, ids: (0,) * len(a.shape))
    slots = pl.BlockSpec((n, SLOTS, width), lambda e, ids: (0, e, 0))
    by_slot = struct(n, PAIR * SLOTS, width)
    by_expert = struct(2 * PAIR, routes, width)
    turned = struct(n, ROWS, 2 * PAIR * SLOTS)
    inner = struct(PAIR, routes, ff)
    act = struct(PAIR, routes, 2 * ff)
    return pl.pallas_call(
        functools.partial(first_kernel, counts, cot_at, len(cots)),
        out_shape=[by_slot, by_slot, by_expert, by_expert, turned, turned, turned, inner, act],
        grid_spec=pltpu.PrefetchScalarGridSpec(
            num_scalar_prefetch=1,
            grid=(PAIR,),
            in_specs=[whole(a) for a in (*tokens, *cots)] + [one_at(gate_up), one_at(down)],
            out_specs=[slots, slots, kept(by_expert), kept(by_expert)]
            + [kept(turned)] * 3
            + [one_at(inner), one_at(act)],
        ),
        compiler_params=pltpu.CompilerParams(dimension_semantics=("arbitrary",)),
        name="first_layer",
    )(ids, *tokens, *cots, gate_up, down)


def last_kernel(n, *refs):
    rows = jnp.concatenate([ref[0] for ref in refs[:n]], axis=0)
    scaled = jnp.concatenate([ref[0] for ref in refs[n : 2 * n]], axis=0)
    gu_ref, dn_ref, out_ref, back_ref, inner_ref, act_ref = refs[2 * n :]
    inner, expert_out, act_grad, route_grad = experts_of(rows, scaled, gu_ref[0], dn_ref[0])
    inner_ref[0] = inner
    act_ref[0] = act_grad
    for b in range(BLOCKS):
        out_ref[b] = expert_out[b * SLOTS : (b + 1) * SLOTS]
        back_ref[b] = route_grad[b * SLOTS : (b + 1) * SLOTS]


def last_layer(rows, scaled, gate_up, down):
    width = gate_up.shape[1]
    ff = down.shape[1]
    routes = BLOCKS * SLOTS
    slots = pl.BlockSpec((BLOCKS, SLOTS, width), lambda e: (0, e, 0))
    by_slot = struct(BLOCKS, PAIR * SLOTS, width)
    inner = struct(PAIR, routes, ff)
    act = struct(PAIR, routes, 2 * ff)
    return pl.pallas_call(
        functools.partial(last_kernel, len(rows)),
        out_shape=[by_slot, by_slot, inner, act],
        grid=(PAIR,),
        in_specs=[one_at(a, PAIR) for a in (*rows, *scaled)] + [one_at(gate_up), one_at(down)],
        out_specs=[slots, slots, one_at(inner), one_at(act)],
        compiler_params=pltpu.CompilerParams(dimension_semantics=("arbitrary",)),
        name="last_layer",
    )(*rows, *scaled, gate_up, down)


MIXED = (4, 2, 2, 2, 2, 2, 2)


def combine_kernel(*refs):
    near, side, far, partner = refs[:5], refs[5:10], refs[10:15], refs[15:17]
    mixed_refs = refs[17 : 17 + len(MIXED)]
    grad_refs = refs[17 + len(MIXED) :]
    mixed_at = [(ref, j) for ref, count in zip(mixed_refs, MIXED) for j in range(count)]
    for group in range(4):

        @pl.when(pl.program_id(0) == group)
        def _():
            outs, backs, sels, highs, lows = (near, side, side, far)[group]
            for j in range(4):
                out = jnp.concatenate([outs[j], partner[0][j]], axis=0)
                back = jnp.concatenate([backs[j], partner[1][j]], axis=0)
                ref, i = mixed_at[4 * group + j]
                ref[i] = (nn(highs[j], out) + nn(lows[j], out)).astype(BF)
                grad_refs[NX * (0, 1, 1, 2)[group] + j][0] = nn(sels[j], back).astype(BF)


def combine(near, side, far, partner):
    width = partner[0].shape[2]
    some = lambda a: pl.BlockSpec((4,) + a.shape[1:], lambda g: (jnp.clip(g - 1, 0, 1), 0, 0))
    once = lambda a: pl.BlockSpec(a.shape, lambda g: (0, 0, 0))
    each = lambda a: pl.BlockSpec((4,) + a.shape[1:], lambda g: (g, 0, 0))
    shapes = [struct(count, ROWS, width) for count in MIXED]
    grads_of = [struct(1, ROWS, width), struct(2, ROWS, width), struct(1, ROWS, width)]
    return pl.pallas_call(
        combine_kernel,
        out_shape=shapes + [a for a in grads_of for _ in range(NX)],
        grid=(4,),
        in_specs=[once(a) for a in near]
        + [some(a) for a in side]
        + [once(a) for a in far]
        + [each(a) for a in partner],
        out_specs=[once(a) for a in shapes]
        + [once(grads_of[0])] * NX
        + [pl.BlockSpec((1, ROWS, width), lambda g: (jnp.clip(g - 1, 0, 1), 0, 0))] * NX
        + [once(grads_of[2])] * NX,
        compiler_params=pltpu.CompilerParams(dimension_semantics=("arbitrary",)),
        name="combine",
    )(*near, *side, *far, *partner)


def grads_kernel(counts, *refs):
    groups = []
    for count in counts:
        groups.append(jnp.concatenate([ref[0] for ref in refs[:count]], axis=0))
        refs = refs[count:]
    rows, scaled, inner, act = groups
    out = refs[-1]
    parts = out.shape[0]
    lanes = out.shape[3]
    tiles = act.shape[1] // lanes
    high = rows.shape[1] // parts
    for d in range(0, parts, 2):
        grad = tn(rows[:, d * high : (d + 2) * high], act).astype(BF)
        for p in range(2):
            for c in range(tiles):
                out[d + p, 0, c * high : (c + 1) * high, :] = grad[
                    p * high : (p + 1) * high, c * lanes : (c + 1) * lanes
                ]
    down = tn(inner, scaled).astype(BF)
    for d in range(parts):
        out[d, 0, tiles * high :, :] = down[:, d * lanes : (d + 1) * lanes]


def grads(rows, scaled, inner, act, parts, first, into=None):
    width = rows[0].shape[2]
    ff = inner[0].shape[2]
    lanes = width // parts
    shape = (parts, 2 * PAIR, lanes * (2 * ff // lanes) + ff, lanes)
    more = [] if into is None else [into]
    operands = [*rows, *scaled, *inner, *act]
    return pl.pallas_call(
        functools.partial(grads_kernel, (len(rows), len(scaled), len(inner), len(act))),
        out_shape=struct(*shape),
        grid=(PAIR,),
        in_specs=[one_at(a, first) for a in (*rows, *scaled)]
        + [one_at(a) for a in (*inner, *act)]
        + [pl.BlockSpec(memory_space=pl.ANY)] * len(more),
        out_specs=pl.BlockSpec((parts, 1) + shape[2:], lambda e: (0, e + first, 0, 0)),
        input_output_aliases={len(operands): 0} if more else {},
        compiler_params=pltpu.CompilerParams(dimension_semantics=("arbitrary",)),
        name="weight_grads",
    )(*operands, *more)


def share_kernel(part_ref, gu_ref, dn_ref, out_ref):
    lanes = out_ref.shape[2]
    tiles = gu_ref.shape[2] // lanes
    high = gu_ref.shape[1]
    for c in range(tiles):
        out_ref[0, c * high : (c + 1) * high, :] = gu_ref[0, :, c * lanes : (c + 1) * lanes]
    out_ref[0, tiles * high :, :] = dn_ref[0]


def share_of(part, gate_up, down, parts):
    lanes = down.shape[2] // parts
    high = gate_up.shape[1] // parts
    rows = high * (gate_up.shape[2] // lanes) + down.shape[1]
    return pl.pallas_call(
        share_kernel,
        out_shape=jax.ShapeDtypeStruct((PAIR, rows, lanes), BF),
        grid_spec=pltpu.PrefetchScalarGridSpec(
            num_scalar_prefetch=1,
            grid=(PAIR,),
            in_specs=[
                pl.BlockSpec((1, high, gate_up.shape[2]), lambda e, part: (e, part[0], 0)),
                pl.BlockSpec((1, down.shape[1], lanes), lambda e, part: (e, 0, part[0])),
            ],
            out_specs=pl.BlockSpec((1, rows, lanes), lambda e, part: (e, 0, 0)),
        ),
        name="share",
    )(part, gate_up, down)


def whole_kernel(in_ref, gu_ref, dn_ref):
    parts = in_ref.shape[0]
    lanes = in_ref.shape[3]
    tiles = gu_ref.shape[2] // lanes
    high = gu_ref.shape[1] // parts
    for d in range(parts):
        for c in range(tiles):
            gu_ref[0, d * high : (d + 1) * high, c * lanes : (c + 1) * lanes] = in_ref[
                d, 0, c * high : (c + 1) * high, :
            ]
        dn_ref[0, :, d * lanes : (d + 1) * lanes] = in_ref[d, 0, tiles * high :, :]


def whole_of(pieces, gate_up, down):
    parts, _, rows, lanes = pieces.shape
    one = lambda shape: pl.BlockSpec((1,) + shape[1:], lambda e: (e, 0, 0))
    return pl.pallas_call(
        whole_kernel,
        out_shape=[jax.ShapeDtypeStruct(a.shape, BF) for a in (gate_up, down)],
        grid=(PAIR,),
        in_specs=[pl.BlockSpec((parts, 1, rows, lanes), lambda e: (0, e, 0, 0))],
        out_specs=[one(gate_up.shape), one(down.shape)],
        name="whole",
    )(pieces)


def give_kernel(flag_ref, in_ref, out_ref):
    out_ref[...] = in_ref[...]


def give_of(flag, mine_of):
    shape = mine_of.shape
    block = (1,) + shape[1:]
    return pl.pallas_call(
        give_kernel,
        out_shape=struct(PAIR, *shape[1:]),
        grid_spec=pltpu.PrefetchScalarGridSpec(
            num_scalar_prefetch=1,
            grid=(PAIR,),
            in_specs=[
                pl.BlockSpec(
                    block,
                    lambda e, flag: (jnp.where(e == 0, PAIR, PAIR + 1 - PAIR * flag[0]), 0, 0),
                )
            ],
            out_specs=pl.BlockSpec(block, lambda e, flag: (e, 0, 0)),
        ),
        name="give",
    )(flag, mine_of)


def finish_kernel(flag_ref, mine_ref, got_ref, gu_ref, dn_ref):
    lanes = gu_ref.shape[1]
    tiles = gu_ref.shape[2] // lanes
    for s in range(PAIR):
        if s == 0:
            keep = mine_ref[0].astype(F32)
        else:
            swapped = flag_ref[0] > 0
            keep = jnp.where(swapped, mine_ref[PAIR + 1].astype(F32), mine_ref[1].astype(F32))
        grad = keep + got_ref[s].astype(F32)
        for c in range(tiles):
            gu_ref[s, :, c * lanes : (c + 1) * lanes] = grad[c * lanes : (c + 1) * lanes, :]
        dn_ref[s] = grad[tiles * lanes :, :]


def finish(flag, mine_of, got, ff):
    lanes = got.shape[2]
    return pl.pallas_call(
        finish_kernel,
        out_shape=[
            jax.ShapeDtypeStruct((PAIR, lanes, 2 * ff), F32),
            jax.ShapeDtypeStruct((PAIR, ff, lanes), F32),
        ],
        in_specs=[
            pl.BlockSpec(memory_space=pltpu.SMEM),
            pl.BlockSpec(memory_space=pltpu.VMEM),
            pl.BlockSpec(memory_space=pltpu.VMEM),
        ],
        out_specs=[pl.BlockSpec(memory_space=pltpu.VMEM)] * 2,
        name="finish",
    )(flag, mine_of, got)


AROUND = (1, -1, 2)


def move(block, dz, dx):
    route = [
        (z * NX + x, (z + dz) % NZ * NX + (x + dx) % NX) for z in range(NZ) for x in range(NX)
    ]
    return lax.ppermute(block, "expert", route)


def total(*arrays):
    acc = arrays[0].astype(F32)
    for a in arrays[1:]:
        acc = acc + a.astype(F32)
    return acc


def step(tokens, cotangent, expert_ids, route_gates, pair_swaps, gate_up, down):
    devices = lax.axis_size("expert")
    parts = lax.axis_size("dp")
    half_axis = devices // 2
    me = lax.axis_index("expert")
    width = tokens.shape[1]
    ff = down.shape[1]
    swapped = (
        jnp.sum(jnp.where(jnp.arange(half_axis) == me % half_axis, pair_swaps % 2, 0)) > 0
    )
    flag = swapped.astype(jnp.int32).reshape(1)
    partner = (me + half_axis) % devices
    ids = jnp.stack([2 * me, 2 * me + 1, 2 * partner, 2 * partner + 1]).astype(jnp.int32)

    cot_up = move(cotangent, 1, 0)
    cot_down = move(cotangent, -1, 0)
    cot_near = [move(cotangent, 0, dx) for dx in AROUND]

    part = lax.axis_index("dp").astype(jnp.int32).reshape(1)
    share = move(share_of(part, gate_up, down, parts), NZ // 2, 0)
    pieces = lax.all_gather(share, "dp", axis=0, tiled=False)

    high = lax.reduce_precision(route_gates, 8, 7)
    rest = route_gates - high
    middle = lax.reduce_precision(rest, 8, 7)
    low = rest - middle
    meta = jnp.concatenate([expert_ids.astype(F32).T, high.T, middle.T, low.T], axis=1)
    meta = jnp.pad(meta.astype(BF), ((0, 0), (0, width - meta.shape[1])))
    block = jnp.concatenate([tokens, meta], axis=0)
    near = jnp.stack([block] + [move(block, 0, dx) for dx in AROUND])
    above = move(near, 1, 0)
    below = move(near, -1, 0)
    far_above = move(above[:FAR], 1, 0)
    far_below = move(below[FAR:], -1, 0)

    cot_far_up = move(cot_up, 1, 0)
    cot_far_down = move(cot_down, -1, 0)
    to_right = jnp.stack([cot_up, cot_down, cot_far_up])
    to_left = jnp.stack([cot_up, cot_down, cot_far_down])
    cot_side = [move(to_right, 0, 1), move(to_left, 0, -1), move(to_left, 0, 2)]
    firsts = []
    for blocks, cots, cot_at in (
        ([near], [cotangent, *cot_near], [(k, None) for k in range(NX)]),
        (
            [above, below],
            [cot_up, cot_down, *cot_side],
            [(k and k + 1, None if k == 0 else 0) for k in range(NX)]
            + [(k + 1, None if k == 0 else 1) for k in range(NX)],
        ),
        (
            [far_above, far_below],
            [cot_far_up, *cot_side],
            [(k, None if k == 0 else 2) for k in range(NX)],
        ),
    ):
        firsts.append(first_layer(ids, blocks, cots, cot_at, gate_up, down))
    rows, scaled = [f[2] for f in firsts], [f[3] for f in firsts]
    weight_grads = grads(
        rows, scaled, [f[7] for f in firsts], [f[8] for f in firsts], parts, 0
    )
    partner_gu, partner_dn = whole_of(pieces, gate_up, down)
    out3, back3, inner3, act3 = last_layer(rows, scaled, partner_gu, partner_dn)
    weight_grads = grads(rows, scaled, (inner3,), (act3,), parts, PAIR, weight_grads)
    mine_of = lax.psum_scatter(weight_grads, "dp", scatter_dimension=0, tiled=False)
    results = combine(*(f[:2] + f[4:7] for f in firsts), (out3, back3))
    near_grads, side_grads, far_grads = (
        results[k : k + NX] for k in range(len(MIXED), len(MIXED) + 3 * NX, NX)
    )

    home = ((1, -1), (2, 1), (3, 2))
    near_back, side_back, far_back = (
        [move(part[k], 0, dx) for k, dx in home]
        for part in (near_grads, side_grads, far_grads)
    )
    near_mix, up_late, up_now, down_now, down_late, far_up, far_down = results[: len(MIXED)]
    back_up = move(far_up, -1, 0)
    back_down = move(far_down, 1, 0)
    up_now = move(up_now, -1, 0)
    down_now = move(down_now, 1, 0)
    up_late = move(total(up_late, back_up).astype(BF), -1, 0)
    down_late = move(total(down_late, back_down).astype(BF), 1, 0)
    low = total(near_mix[:FAR], up_late, down_now)
    top = total(near_mix[FAR:], up_now, down_late)
    mixed = (
        low[0]
        + move(low[1].astype(BF), 0, -1).astype(F32)
        + move(top[0].astype(BF), 0, 1).astype(F32)
        + move(top[1].astype(BF), 0, 2).astype(F32)
    ).astype(BF)

    grad_far_up = move(total(far_grads[0][0], far_back[0][0]).astype(BF), -1, 0)
    grad_far_down = move(total(far_back[1][0], far_back[2][0]).astype(BF), 1, 0)
    sides = [side_grads[0], *side_back]
    grad_up = total(*[a[0] for a in sides], grad_far_up).astype(BF)
    grad_down_z = total(*[a[1] for a in sides], grad_far_down).astype(BF)
    last_up = move(grad_up, -1, 0)
    last_down = move(grad_down_z, 1, 0)
    grad_tokens = total(near_grads[0][0], *[a[0] for a in near_back], last_up, last_down).astype(BF)

    moved_gate_up = jnp.stack([gate_up[0], jnp.where(swapped, partner_gu[1], gate_up[1])])
    moved_down = jnp.stack([down[0], jnp.where(swapped, partner_dn[1], down[1])])

    give = give_of(flag, mine_of)
    got = move(give, NZ // 2, 0)
    grad_gate_up, grad_down = finish(flag, mine_of, got, ff)
    return (mixed, grad_tokens, moved_gate_up, moved_down, grad_gate_up, grad_down)


def solution(mesh):
    in_specs = (
        P(("expert", "dp"), None),
        P(("expert", "dp"), None),
        P(("expert", "dp"), None),
        P(("expert", "dp"), None),
        P(),
        P("expert", None, None),
        P("expert", None, None),
    )
    out_specs = (
        P(("expert", "dp"), None),
        P(("expert", "dp"), None),
        P("expert", None, None),
        P("expert", None, None),
        P("expert", "dp", None),
        P("expert", None, "dp"),
    )
    return jax.shard_map(step, mesh=mesh, in_specs=in_specs, out_specs=out_specs, check_vma=False)
```

```python
import functools

import jax
import jax.numpy as jnp
from jax import lax
from jax.experimental import pallas as pl
from jax.experimental.pallas import tpu as pltpu
from jax.sharding import PartitionSpec as P


BF = jnp.bfloat16
F32 = jnp.float32
ROWS = 128
SLOTS = 32
META = 8
NX = 4
NZ = 8
PAIR = 2


def nt(a, b):
    return lax.dot_general(a, b, (((1,), (1,)), ((), ())), preferred_element_type=F32)


def tn(a, b):
    return lax.dot_general(a, b, (((0,), (0,)), ((), ())), preferred_element_type=F32)


def nn(a, b):
    return lax.dot_general(a, b, (((1,), (0,)), ((), ())), preferred_element_type=F32)


NEAR, SIDE, FAR = 4, 4, 2
BLOCKS = NEAR + 2 * SIDE + 2 * FAR


def constants():
    upper = lax.broadcasted_iota(jnp.int32, (ROWS, ROWS), 0) <= lax.broadcasted_iota(
        jnp.int32, (ROWS, ROWS), 1
    )
    slot_no = lax.broadcasted_iota(jnp.int32, (SLOTS, ROWS), 0).astype(F32) + 1.0
    return upper.astype(BF), slot_no


def picks_of(meta, ids_ref, experts, upper, slot_no):
    meta = meta.astype(F32)
    named = meta[:, 0:ROWS]
    gates = (meta[:, ROWS : 2 * ROWS] + meta[:, 2 * ROWS : 3 * ROWS]) + meta[:, 3 * ROWS :]
    hits = []
    weights = []
    for h in experts:
        equal = named == ids_ref[h].astype(F32)
        hits.append(jnp.sum(jnp.where(equal, 1.0, 0.0), axis=0, keepdims=True))
        weights.append(jnp.sum(jnp.where(equal, gates, 0.0), axis=0, keepdims=True))
    rank = nn(jnp.concatenate(hits * (8 // len(hits)), axis=0).astype(BF), upper)
    picks = [
        jnp.where((rank[h : h + 1, :] == slot_no) & (hit > 0.0), 1.0, 0.0)
        for h, hit in enumerate(hits)
    ]
    scales = [pick * weight for pick, weight in zip(picks, weights)]
    return jnp.concatenate(picks, axis=0), jnp.concatenate(scales, axis=0)


def experts_of(rows_in, scaled_cot, gu, dn):
    ff = dn.shape[0]
    activation = nn(rows_in, gu)
    inner_grad = nt(scaled_cot, dn)
    gate_part = activation[:, :ff]
    up_part = activation[:, ff:]
    sigmoid_gate = jax.nn.sigmoid(gate_part)
    silu_gate = gate_part * sigmoid_gate
    inner = (silu_gate * up_part).astype(BF)
    expert_out = nn(inner, dn).astype(BF)
    gate_grad = inner_grad * up_part * sigmoid_gate * (1.0 + gate_part * (1.0 - sigmoid_gate))
    act_grad = jnp.concatenate([gate_grad, inner_grad * silu_gate], axis=1).astype(BF)
    route_grad = nt(act_grad, gu).astype(BF)
    return inner, expert_out, act_grad, route_grad


def first_kernel(counts, cot_at, n_cots, ids_ref, *refs):
    token_refs = refs[: len(counts)]
    cots = refs[len(counts) : len(counts) + n_cots]
    refs = refs[len(counts) + n_cots :]
    gu_ref, dn_ref, out_ref, back_ref, rows_ref, scaled_ref = refs[:6]
    sel_ref, high_ref, low_ref, inner_ref, act_ref = refs[6:]
    e = pl.program_id(0)
    tokens_at = [(ref, j) for ref, count in zip(token_refs, counts) for j in range(count)]

    @pl.when(e == 0)
    def _():
        upper, slot_no = constants()
        for b, (ref, j) in enumerate(tokens_at):
            meta = ref[j, ROWS : ROWS + META, 0 : 4 * ROWS]
            select, scale = picks_of(meta, ids_ref, range(2 * PAIR), upper, slot_no)
            select_bf = select.astype(BF)
            k, i = cot_at[b]
            cot_rows = cots[k][...] if i is None else cots[k][i]
            rows = nn(select_bf, ref[j, 0:ROWS, :]).astype(BF)
            cot = nn(select_bf, cot_rows)
            scaled = (jnp.sum(scale, axis=1, keepdims=True) * cot).astype(BF)
            for h in range(2 * PAIR):
                rows_ref[h, b * SLOTS : (b + 1) * SLOTS, :] = rows[h * SLOTS : (h + 1) * SLOTS]
                scaled_ref[h, b * SLOTS : (b + 1) * SLOTS, :] = scaled[h * SLOTS : (h + 1) * SLOTS]
            scale_t = scale.T
            high = scale_t.astype(BF)
            sel_ref[b] = select.T.astype(BF)
            high_ref[b] = high
            low_ref[b] = (scale_t - high.astype(F32)).astype(BF)

    inner, expert_out, act_grad, route_grad = experts_of(
        rows_ref[e], scaled_ref[e], gu_ref[0], dn_ref[0]
    )
    inner_ref[0] = inner
    act_ref[0] = act_grad
    for b in range(len(tokens_at)):
        out_ref[b] = expert_out[b * SLOTS : (b + 1) * SLOTS]
        back_ref[b] = route_grad[b * SLOTS : (b + 1) * SLOTS]


def one_at(a, shift=0):
    return pl.BlockSpec((1,) + a.shape[1:], lambda e, *_: (e + shift, 0, 0))


def struct(*shape):
    return jax.ShapeDtypeStruct(shape, BF)


def first_layer(ids, tokens, cots, cot_at, gate_up, down):
    width = tokens[0].shape[2]
    ff = down.shape[1]
    counts = tuple(a.shape[0] for a in tokens)
    n = sum(counts)
    routes = n * SLOTS
    whole = lambda a: pl.BlockSpec(
        a.shape, lambda e, ids: (0,) * len(a.shape), pipeline_mode=pl.Buffered(1)
    )
    kept = lambda a: pl.BlockSpec(a.shape, lambda e, ids: (0,) * len(a.shape))
    slots = pl.BlockSpec((n, SLOTS, width), lambda e, ids: (0, e, 0))
    by_slot = struct(n, PAIR * SLOTS, width)
    by_expert = struct(2 * PAIR, routes, width)
    turned = struct(n, ROWS, 2 * PAIR * SLOTS)
    inner = struct(PAIR, routes, ff)
    act = struct(PAIR, routes, 2 * ff)
    return pl.pallas_call(
        functools.partial(first_kernel, counts, cot_at, len(cots)),
        out_shape=[by_slot, by_slot, by_expert, by_expert, turned, turned, turned, inner, act],
        grid_spec=pltpu.PrefetchScalarGridSpec(
            num_scalar_prefetch=1,
            grid=(PAIR,),
            in_specs=[whole(a) for a in (*tokens, *cots)] + [one_at(gate_up), one_at(down)],
            out_specs=[slots, slots, kept(by_expert), kept(by_expert)]
            + [kept(turned)] * 3
            + [one_at(inner), one_at(act)],
        ),
        compiler_params=pltpu.CompilerParams(dimension_semantics=("arbitrary",)),
        name="first_layer",
    )(ids, *tokens, *cots, gate_up, down)


def last_kernel(n, *refs):
    rows = jnp.concatenate([ref[0] for ref in refs[:n]], axis=0)
    scaled = jnp.concatenate([ref[0] for ref in refs[n : 2 * n]], axis=0)
    pieces_ref, out_ref, back_ref, inner_ref, act_ref, gu_ref, dn_ref = refs[2 * n :]
    whole_kernel(pieces_ref, gu_ref, dn_ref)
    inner, expert_out, act_grad, route_grad = experts_of(rows, scaled, gu_ref[0], dn_ref[0])
    inner_ref[0] = inner
    act_ref[0] = act_grad
    for b in range(BLOCKS):
        out_ref[b] = expert_out[b * SLOTS : (b + 1) * SLOTS]
        back_ref[b] = route_grad[b * SLOTS : (b + 1) * SLOTS]


def last_layer(rows, scaled, pieces, gate_up, down):
    width = gate_up.shape[1]
    ff = down.shape[1]
    routes = BLOCKS * SLOTS
    slots = pl.BlockSpec((BLOCKS, SLOTS, width), lambda e: (0, e, 0))
    by_slot = struct(BLOCKS, PAIR * SLOTS, width)
    inner = struct(PAIR, routes, ff)
    act = struct(PAIR, routes, 2 * ff)
    return pl.pallas_call(
        functools.partial(last_kernel, len(rows)),
        out_shape=[by_slot, by_slot, inner, act],
        grid=(PAIR,),
        in_specs=[one_at(a, PAIR) for a in (*rows, *scaled)]
        + [pl.BlockSpec((pieces.shape[0], 1) + pieces.shape[2:], lambda e: (0, e, 0, 0))],
        out_specs=[slots, slots, one_at(inner), one_at(act)],
        scratch_shapes=[pltpu.VMEM((1,) + a.shape[1:], BF) for a in (gate_up, down)],
        compiler_params=pltpu.CompilerParams(dimension_semantics=("arbitrary",)),
        name="last_layer",
    )(*rows, *scaled, pieces)


MIXED = (4, 2, 2, 2, 2, 2, 2)


def combine_kernel(*refs):
    near, side, far, partner = refs[:5], refs[5:10], refs[10:15], refs[15:17]
    mixed_refs = refs[17 : 17 + len(MIXED)]
    grad_refs = refs[17 + len(MIXED) :]
    mixed_at = [(ref, j) for ref, count in zip(mixed_refs, MIXED) for j in range(count)]
    for group in range(4):

        @pl.when(pl.program_id(0) == group)
        def _():
            outs, backs, sels, highs, lows = (near, side, side, far)[group]
            for j in range(4):
                out = jnp.concatenate([outs[j], partner[0][j]], axis=0)
                back = jnp.concatenate([backs[j], partner[1][j]], axis=0)
                ref, i = mixed_at[4 * group + j]
                ref[i] = (nn(highs[j], out) + nn(lows[j], out)).astype(BF)
                grad_refs[NX * (0, 1, 1, 2)[group] + j][0] = nn(sels[j], back).astype(BF)


def combine(near, side, far, partner):
    width = partner[0].shape[2]
    some = lambda a: pl.BlockSpec((4,) + a.shape[1:], lambda g: (jnp.clip(g - 1, 0, 1), 0, 0))
    once = lambda a: pl.BlockSpec(a.shape, lambda g: (0, 0, 0))
    each = lambda a: pl.BlockSpec((4,) + a.shape[1:], lambda g: (g, 0, 0))
    shapes = [struct(count, ROWS, width) for count in MIXED]
    grads_of = [struct(1, ROWS, width), struct(2, ROWS, width), struct(1, ROWS, width)]
    return pl.pallas_call(
        combine_kernel,
        out_shape=shapes + [a for a in grads_of for _ in range(NX)],
        grid=(4,),
        in_specs=[once(a) for a in near]
        + [some(a) for a in side]
        + [once(a) for a in far]
        + [each(a) for a in partner],
        out_specs=[once(a) for a in shapes]
        + [once(grads_of[0])] * NX
        + [pl.BlockSpec((1, ROWS, width), lambda g: (jnp.clip(g - 1, 0, 1), 0, 0))] * NX
        + [once(grads_of[2])] * NX,
        compiler_params=pltpu.CompilerParams(dimension_semantics=("arbitrary",)),
        name="combine",
    )(*near, *side, *far, *partner)


def grads_kernel(counts, *refs):
    groups = []
    for count in counts:
        groups.append(jnp.concatenate([ref[0] for ref in refs[:count]], axis=0))
        refs = refs[count:]
    rows, scaled, inner, act = groups
    out = refs[-1]
    parts = out.shape[0]
    lanes = out.shape[3]
    tiles = act.shape[1] // lanes
    high = rows.shape[1] // parts
    for d in range(0, parts, 2):
        grad = tn(rows[:, d * high : (d + 2) * high], act).astype(BF)
        for p in range(2):
            for c in range(tiles):
                out[d + p, 0, c * high : (c + 1) * high, :] = grad[
                    p * high : (p + 1) * high, c * lanes : (c + 1) * lanes
                ]
    down = tn(inner, scaled).astype(BF)
    for d in range(parts):
        out[d, 0, tiles * high :, :] = down[:, d * lanes : (d + 1) * lanes]


def grads(rows, scaled, inner, act, parts, first, into=None):
    width = rows[0].shape[2]
    ff = inner[0].shape[2]
    lanes = width // parts
    shape = (parts, 2 * PAIR, lanes * (2 * ff // lanes) + ff, lanes)
    more = [] if into is None else [into]
    operands = [*rows, *scaled, *inner, *act]
    return pl.pallas_call(
        functools.partial(grads_kernel, (len(rows), len(scaled), len(inner), len(act))),
        out_shape=struct(*shape),
        grid=(PAIR,),
        in_specs=[one_at(a, first) for a in (*rows, *scaled)]
        + [one_at(a) for a in (*inner, *act)]
        + [pl.BlockSpec(memory_space=pl.ANY)] * len(more),
        out_specs=pl.BlockSpec((parts, 1) + shape[2:], lambda e: (0, e + first, 0, 0)),
        input_output_aliases={len(operands): 0} if more else {},
        compiler_params=pltpu.CompilerParams(dimension_semantics=("arbitrary",)),
        name="weight_grads",
    )(*operands, *more)


def share_kernel(part_ref, gu_ref, dn_ref, out_ref):
    lanes = out_ref.shape[2]
    tiles = gu_ref.shape[2] // lanes
    high = gu_ref.shape[1]
    for c in range(tiles):
        out_ref[0, c * high : (c + 1) * high, :] = gu_ref[0, :, c * lanes : (c + 1) * lanes]
    out_ref[0, tiles * high :, :] = dn_ref[0]


def share_of(part, gate_up, down, parts):
    lanes = down.shape[2] // parts
    high = gate_up.shape[1] // parts
    rows = high * (gate_up.shape[2] // lanes) + down.shape[1]
    return pl.pallas_call(
        share_kernel,
        out_shape=jax.ShapeDtypeStruct((PAIR, rows, lanes), BF),
        grid_spec=pltpu.PrefetchScalarGridSpec(
            num_scalar_prefetch=1,
            grid=(PAIR,),
            in_specs=[
                pl.BlockSpec((1, high, gate_up.shape[2]), lambda e, part: (e, part[0], 0)),
                pl.BlockSpec((1, down.shape[1], lanes), lambda e, part: (e, 0, part[0])),
            ],
            out_specs=pl.BlockSpec((1, rows, lanes), lambda e, part: (e, 0, 0)),
        ),
        name="share",
    )(part, gate_up, down)


def whole_kernel(in_ref, gu_ref, dn_ref):
    parts = in_ref.shape[0]
    lanes = in_ref.shape[3]
    tiles = gu_ref.shape[2] // lanes
    high = gu_ref.shape[1] // parts
    for d in range(parts):
        for c in range(tiles):
            gu_ref[0, d * high : (d + 1) * high, c * lanes : (c + 1) * lanes] = in_ref[
                d, 0, c * high : (c + 1) * high, :
            ]
        dn_ref[0, :, d * lanes : (d + 1) * lanes] = in_ref[d, 0, tiles * high :, :]


def whole_of(pieces, gate_up, down):
    parts, _, rows, lanes = pieces.shape
    one = lambda shape: pl.BlockSpec((1,) + shape[1:], lambda e: (e, 0, 0))
    return pl.pallas_call(
        whole_kernel,
        out_shape=[jax.ShapeDtypeStruct(a.shape, BF) for a in (gate_up, down)],
        grid=(PAIR,),
        in_specs=[pl.BlockSpec((parts, 1, rows, lanes), lambda e: (0, e, 0, 0))],
        out_specs=[one(gate_up.shape), one(down.shape)],
        name="whole",
    )(pieces)


def give_kernel(flag_ref, in_ref, out_ref):
    out_ref[...] = in_ref[...]


def give_of(flag, mine_of):
    shape = mine_of.shape
    block = (1,) + shape[1:]
    return pl.pallas_call(
        give_kernel,
        out_shape=struct(PAIR, *shape[1:]),
        grid_spec=pltpu.PrefetchScalarGridSpec(
            num_scalar_prefetch=1,
            grid=(PAIR,),
            in_specs=[
                pl.BlockSpec(
                    block,
                    lambda e, flag: (jnp.where(e == 0, PAIR, PAIR + 1 - PAIR * flag[0]), 0, 0),
                )
            ],
            out_specs=pl.BlockSpec(block, lambda e, flag: (e, 0, 0)),
        ),
        name="give",
    )(flag, mine_of)


def finish_kernel(flag_ref, mine_ref, got_ref, gu_ref, dn_ref):
    lanes = gu_ref.shape[1]
    tiles = gu_ref.shape[2] // lanes
    for s in range(PAIR):
        if s == 0:
            keep = mine_ref[0].astype(F32)
        else:
            swapped = flag_ref[0] > 0
            keep = jnp.where(swapped, mine_ref[PAIR + 1].astype(F32), mine_ref[1].astype(F32))
        grad = keep + got_ref[s].astype(F32)
        for c in range(tiles):
            gu_ref[s, :, c * lanes : (c + 1) * lanes] = grad[c * lanes : (c + 1) * lanes, :]
        dn_ref[s] = grad[tiles * lanes :, :]


def finish(flag, mine_of, got, ff):
    lanes = got.shape[2]
    return pl.pallas_call(
        finish_kernel,
        out_shape=[
            jax.ShapeDtypeStruct((PAIR, lanes, 2 * ff), F32),
            jax.ShapeDtypeStruct((PAIR, ff, lanes), F32),
        ],
        in_specs=[
            pl.BlockSpec(memory_space=pltpu.SMEM),
            pl.BlockSpec(memory_space=pltpu.VMEM),
            pl.BlockSpec(memory_space=pltpu.VMEM),
        ],
        out_specs=[pl.BlockSpec(memory_space=pltpu.VMEM)] * 2,
        name="finish",
    )(flag, mine_of, got)


AROUND = (1, -1, 2)


def move(block, dz, dx):
    route = [
        (z * NX + x, (z + dz) % NZ * NX + (x + dx) % NX) for z in range(NZ) for x in range(NX)
    ]
    return lax.ppermute(block, "expert", route)


def total(*arrays):
    acc = arrays[0].astype(F32)
    for a in arrays[1:]:
        acc = acc + a.astype(F32)
    return acc


def step(tokens, cotangent, expert_ids, route_gates, pair_swaps, gate_up, down):
    devices = lax.axis_size("expert")
    parts = lax.axis_size("dp")
    half_axis = devices // 2
    me = lax.axis_index("expert")
    width = tokens.shape[1]
    ff = down.shape[1]
    swapped = (
        jnp.sum(jnp.where(jnp.arange(half_axis) == me % half_axis, pair_swaps % 2, 0)) > 0
    )
    flag = swapped.astype(jnp.int32).reshape(1)
    partner = (me + half_axis) % devices
    ids = jnp.stack([2 * me, 2 * me + 1, 2 * partner, 2 * partner + 1]).astype(jnp.int32)

    cot_up = move(cotangent, 1, 0)
    cot_down = move(cotangent, -1, 0)
    cot_near = [move(cotangent, 0, dx) for dx in AROUND]

    part = lax.axis_index("dp").astype(jnp.int32).reshape(1)
    share = move(share_of(part, gate_up, down, parts), NZ // 2, 0)
    pieces = lax.all_gather(share, "dp", axis=0, tiled=False)

    high = lax.reduce_precision(route_gates, 8, 7)
    rest = route_gates - high
    middle = lax.reduce_precision(rest, 8, 7)
    low = rest - middle
    meta = jnp.concatenate([expert_ids.astype(F32).T, high.T, middle.T, low.T], axis=1)
    meta = jnp.pad(meta.astype(BF), ((0, 0), (0, width - meta.shape[1])))
    block = jnp.concatenate([tokens, meta], axis=0)
    near = jnp.stack([block] + [move(block, 0, dx) for dx in AROUND])
    above = move(near, 1, 0)
    below = move(near, -1, 0)
    far_above = move(above[:FAR], 1, 0)
    far_below = move(below[FAR:], -1, 0)

    cot_far_up = move(cot_up, 1, 0)
    cot_far_down = move(cot_down, -1, 0)
    to_right = jnp.stack([cot_up, cot_down, cot_far_up])
    to_left = jnp.stack([cot_up, cot_down, cot_far_down])
    cot_side = [move(to_right, 0, 1), move(to_left, 0, -1), move(to_left, 0, 2)]
    firsts = []
    for blocks, cots, cot_at in (
        ([near], [cotangent, *cot_near], [(k, None) for k in range(NX)]),
        (
            [above, below],
            [cot_up, cot_down, *cot_side],
            [(k and k + 1, None if k == 0 else 0) for k in range(NX)]
            + [(k + 1, None if k == 0 else 1) for k in range(NX)],
        ),
        (
            [far_above, far_below],
            [cot_far_up, *cot_side],
            [(k, None if k == 0 else 2) for k in range(NX)],
        ),
    ):
        firsts.append(first_layer(ids, blocks, cots, cot_at, gate_up, down))
    rows, scaled = [f[2] for f in firsts], [f[3] for f in firsts]
    weight_grads = grads(
        rows, scaled, [f[7] for f in firsts], [f[8] for f in firsts], parts, 0
    )
    partner_gu, partner_dn = whole_of(pieces, gate_up, down)
    out3, back3, inner3, act3 = last_layer(rows, scaled, pieces, gate_up, down)
    weight_grads = grads(rows, scaled, (inner3,), (act3,), parts, PAIR, weight_grads)
    mine_of = lax.psum_scatter(weight_grads, "dp", scatter_dimension=0, tiled=False)
    results = combine(*(f[:2] + f[4:7] for f in firsts), (out3, back3))
    near_grads, side_grads, far_grads = (
        results[k : k + NX] for k in range(len(MIXED), len(MIXED) + 3 * NX, NX)
    )

    home = ((1, -1), (2, 1), (3, 2))
    near_back, side_back, far_back = (
        [move(part[k], 0, dx) for k, dx in home]
        for part in (near_grads, side_grads, far_grads)
    )
    near_mix, up_late, up_now, down_now, down_late, far_up, far_down = results[: len(MIXED)]
    back_up = move(far_up, -1, 0)
    back_down = move(far_down, 1, 0)
    up_now = move(up_now, -1, 0)
    down_now = move(down_now, 1, 0)
    up_late = move(total(up_late, back_up).astype(BF), -1, 0)
    down_late = move(total(down_late, back_down).astype(BF), 1, 0)
    low = total(near_mix[:FAR], up_late, down_now)
    top = total(near_mix[FAR:], up_now, down_late)
    mixed = (
        low[0]
        + move(low[1].astype(BF), 0, -1).astype(F32)
        + move(top[0].astype(BF), 0, 1).astype(F32)
        + move(top[1].astype(BF), 0, 2).astype(F32)
    ).astype(BF)

    grad_far_up = move(total(far_grads[0][0], far_back[0][0]).astype(BF), -1, 0)
    grad_far_down = move(total(far_back[1][0], far_back[2][0]).astype(BF), 1, 0)
    sides = [side_grads[0], *side_back]
    grad_up = total(*[a[0] for a in sides], grad_far_up).astype(BF)
    grad_down_z = total(*[a[1] for a in sides], grad_far_down).astype(BF)
    last_up = move(grad_up, -1, 0)
    last_down = move(grad_down_z, 1, 0)
    grad_tokens = total(near_grads[0][0], *[a[0] for a in near_back], last_up, last_down).astype(BF)

    moved_gate_up = jnp.stack([gate_up[0], jnp.where(swapped, partner_gu[1], gate_up[1])])
    moved_down = jnp.stack([down[0], jnp.where(swapped, partner_dn[1], down[1])])

    give = give_of(flag, mine_of)
    got = move(give, NZ // 2, 0)
    grad_gate_up, grad_down = finish(flag, mine_of, got, ff)
    return (mixed, grad_tokens, moved_gate_up, moved_down, grad_gate_up, grad_down)


def solution(mesh):
    in_specs = (
        P(("expert", "dp"), None),
        P(("expert", "dp"), None),
        P(("expert", "dp"), None),
        P(("expert", "dp"), None),
        P(),
        P("expert", None, None),
        P("expert", None, None),
    )
    out_specs = (
        P(("expert", "dp"), None),
        P(("expert", "dp"), None),
        P("expert", None, None),
        P("expert", None, None),
        P("expert", "dp", None),
        P("expert", None, "dp"),
    )
    return jax.shard_map(step, mesh=mesh, in_specs=in_specs, out_specs=out_specs, check_vma=False)
```
